256 devices in a mesh: dp: 4 (over x), psg: 64 (over y, z, core).
Axes of the slice: x: 4, y: 4, z: 8, core: 2. Of those that a mesh axis runs over, the one named last changes fastest.
Arguments:
- queries: bfloat16 [4, 128, 2048], P('dp', None, 'psg'), may hold values from -4 to 4
- keys: bfloat16 [4, 128, 256, 2048], P('dp', 'psg'), may hold values from -4 to 4
- values: bfloat16 [4, 128, 256, 2048], P('dp', 'psg'), may hold values from -6 to 6
- lengths: int32 [4, 128], P('dp', 'psg'), may hold values from 16 to 256, as said below
- out_weight: bfloat16 [4096, 2048], P('psg'), may hold values from -0.125 to 0.125
- out_cotangent: bfloat16 [4, 128, 4096], P('dp', None, 'psg'), may hold values from -6 to 6
Outputs:
- layer_out: bfloat16 [4, 128, 4096], P('dp', None, 'psg')
- weight_grad: float32 [4096, 2048], P('psg')
- query_grad: bfloat16 [4, 128, 2048], P('dp', None, 'psg')
- key_grad: bfloat16 [4, 128, 256, 2048], P('dp', 'psg')
- value_grad: bfloat16 [4, 128, 256, 2048], P('dp', 'psg')
The draws below stay inside these ranges and needn't reach their ends.
Inputs may be any that keep to these rules, and one draw needn't show every extreme that they name: `lengths`: every passage has at least 16 valid tokens, counted from its start; in every question some passage has all 256.
All inputs are finite; a program needn't handle non-finite values.
Results may differ from the reference program's by a relative error of at most 0.025.
Values may be sent and summed in bfloat16 or wider, within the bound.
A program may use at most 64 MiB of HBM per device.

```python
import jax
import jax.numpy as jnp
from jax import lax

MODEL_DIM = 4096
HEAD_COUNT = 32
HEAD_SIZE = 64
ANSWER_LEN = 128
PASSAGE_LEN = 256
INNER_DIM = 2048
QUESTIONS = 4
PASSAGES = 128


def paired_draw(key):
    base_key = jax.random.fold_in(key, 11)
    query_key, keys_key, scale_key = jax.random.split(base_key, 3)
    query_shape = (QUESTIONS, ANSWER_LEN, INNER_DIM)
    key_shape = (QUESTIONS, PASSAGES, PASSAGE_LEN, INNER_DIM)
    query_draw = 0.45 * jax.random.normal(query_key, query_shape, jnp.float32)
    key_draw = 0.45 * jax.random.normal(keys_key, key_shape, jnp.float32)
    scales = jnp.exp(jax.random.uniform(scale_key, (QUESTIONS, PASSAGES, PASSAGE_LEN, 1), jnp.float32, -0.5, 0.5))
    query_draw = jnp.clip(query_draw, -4.0, 4.0)
    key_draw = jnp.clip(key_draw * scales, -4.0, 4.0)
    return (query_draw, key_draw)


def draw_queries(key, part):
    return paired_draw(key)[0].astype(jnp.bfloat16)


def draw_keys(key, part):
    return paired_draw(key)[1].astype(jnp.bfloat16)


def draw_lengths(key, part):
    base_key = jax.random.fold_in(key, 23)
    first_key, second_key = jax.random.split(base_key, 2)
    drawn_lengths = jax.random.randint(first_key, (QUESTIONS, PASSAGES), 16, PASSAGE_LEN + 1)
    full_one = jax.random.randint(second_key, (QUESTIONS,), 0, PASSAGES)
    full_marks = jnp.arange(PASSAGES, dtype=jnp.int32)[None, :] == full_one[:, None]
    return jnp.where(full_marks, PASSAGE_LEN, drawn_lengths).astype(jnp.int32)


def level_of(stream_key, dims, cuts, low, top_value):
    def one(dim, blocks):
        draws = jax.random.uniform(jax.random.fold_in(jax.random.fold_in(stream_key, 6), dim), (blocks,), jnp.float32, low / len(cuts), top_value / len(cuts))
        return jnp.repeat(jnp.exp(draws), dims[dim] // blocks).reshape((-1,) + (1,) * (len(dims) - dim - 1))

    factor_of = one(*cuts[0])
    for cut in cuts[1:]:
        factor_of = factor_of * one(*cut)
    return factor_of


def gaussian(key, dims, scale, bound, shards=(), kind=jnp.bfloat16):
    drawn = jax.random.normal(key, dims, jnp.float32) * scale
    if len(shards) > 0:
        drawn = level_of(key, dims, shards, -0.22, 0.18) * drawn
    return jnp.clip(drawn, min=-bound, max=bound).astype(kind)


def setup_inputs(seed: int = 0) -> dict:
    key_of = jax.random.split(jax.random.key(seed), 7)
    queries = draw_queries(jax.random.fold_in(key_of[6], 71), 0)
    keys = draw_keys(jax.random.fold_in(key_of[6], 71), 0)
    values = gaussian(key_of[2], (QUESTIONS, PASSAGES, PASSAGE_LEN, INNER_DIM), 1.0, 6.0, ((0, 4), (1, 64)))
    lengths = draw_lengths(jax.random.fold_in(key_of[6], 71), 0)
    out_weight = gaussian(key_of[4], (MODEL_DIM, INNER_DIM), INNER_DIM ** -0.5, 0.125, ((0, 64),))
    out_cotangent = gaussian(key_of[5], (QUESTIONS, ANSWER_LEN, MODEL_DIM), 1.0, 6.0, ((0, 4), (2, 64)))
    return dict(queries=queries, keys=keys, values=values, lengths=lengths, out_weight=out_weight, out_cotangent=out_cotangent)


def head_slice(block, head_index):
    return lax.dynamic_slice_in_dim(block, head_index * HEAD_SIZE, HEAD_SIZE, 1)


def reference(queries, keys, values, lengths, out_weight, out_cotangent):
    question_count = queries.shape[0]
    key_count = PASSAGES * PASSAGE_LEN
    positions = jnp.arange(PASSAGE_LEN, dtype=jnp.int32)
    valid = (positions[None, None, :] < lengths[:, :, None]).reshape(question_count, key_count)
    keys_flat = keys.reshape(question_count, key_count, INNER_DIM)
    values_flat = values.reshape(question_count, key_count, INNER_DIM)
    head_ids = jnp.arange(HEAD_COUNT, dtype=jnp.int32)

    def forward_one(block):
        query_block, key_block, value_block, valid_block = block

        def one_head(head_index):
            query_head = head_slice(query_block, head_index)
            key_head = head_slice(key_block, head_index)
            value_head = head_slice(value_block, head_index)
            scores = jnp.dot(query_head, key_head.T, preferred_element_type=jnp.float32)
            row_max = jnp.max(jnp.where(valid_block[None, :], scores, -jnp.inf), axis=1)
            weights = jnp.where(valid_block[None, :], jnp.exp(scores - row_max[:, None]), 0.0)
            row_sum = jnp.sum(weights, axis=1)
            output = jnp.dot(weights.astype(jnp.bfloat16), value_head, preferred_element_type=jnp.float32) / row_sum[:, None]
            return output, row_max, row_sum

        output, row_max, row_sum = lax.map(one_head, head_ids)
        return jnp.transpose(output, (1, 0, 2)).reshape(ANSWER_LEN, INNER_DIM), row_max, row_sum

    output, row_max, row_sum = lax.map(forward_one, (queries, keys_flat, values_flat, valid))
    context = output.astype(jnp.bfloat16)
    context_rows = context.reshape(question_count * ANSWER_LEN, INNER_DIM)
    grad_rows = out_cotangent.reshape(question_count * ANSWER_LEN, MODEL_DIM)
    layer_out = jnp.dot(context_rows, out_weight.T, preferred_element_type=jnp.float32).astype(jnp.bfloat16)
    layer_out = layer_out.reshape(question_count, ANSWER_LEN, MODEL_DIM)
    weight_grad = jnp.dot(grad_rows.T, context_rows, preferred_element_type=jnp.float32)
    context_grad = jnp.dot(grad_rows, out_weight, preferred_element_type=jnp.float32).astype(jnp.bfloat16)
    context_grad = context_grad.reshape(question_count, ANSWER_LEN, INNER_DIM)
    products = context_grad.astype(jnp.float32) * context.astype(jnp.float32)
    row_dots = jnp.transpose(jnp.sum(products.reshape(question_count, ANSWER_LEN, HEAD_COUNT, HEAD_SIZE), axis=3), (0, 2, 1))

    def backward_one(block):
        query_block, key_block, value_block, valid_block, grad_block, max_block, sum_block, dots_block = block

        def one_head(head_index):
            query_head = head_slice(query_block, head_index)
            key_head = head_slice(key_block, head_index)
            value_head = head_slice(value_block, head_index)
            grad_head = head_slice(grad_block, head_index)
            scores = jnp.dot(query_head, key_head.T, preferred_element_type=jnp.float32)
            probs = jnp.where(valid_block[None, :], jnp.exp(scores - max_block[head_index][:, None]) / sum_block[head_index][:, None], 0.0)
            prob_grad = jnp.dot(grad_head, value_head.T, preferred_element_type=jnp.float32)
            score_grad = (probs * (prob_grad - dots_block[head_index][:, None])).astype(jnp.bfloat16)
            value_part = jnp.dot(probs.astype(jnp.bfloat16).T, grad_head, preferred_element_type=jnp.float32).astype(jnp.bfloat16)
            key_part = jnp.dot(score_grad.T, query_head, preferred_element_type=jnp.float32).astype(jnp.bfloat16)
            query_part = jnp.dot(score_grad, key_head, preferred_element_type=jnp.float32).astype(jnp.bfloat16)
            return query_part, key_part, value_part

        query_part, key_part, value_part = lax.map(one_head, head_ids)
        query_part = jnp.transpose(query_part, (1, 0, 2)).reshape(ANSWER_LEN, INNER_DIM)
        key_part = jnp.transpose(key_part, (1, 0, 2)).reshape(key_count, INNER_DIM)
        value_part = jnp.transpose(value_part, (1, 0, 2)).reshape(key_count, INNER_DIM)
        return query_part, key_part, value_part

    query_grad, key_grad, value_grad = lax.map(backward_one, (queries, keys_flat, values_flat, valid, context_grad, row_max, row_sum, row_dots))
    key_grad = key_grad.reshape(keys.shape)
    value_grad = value_grad.reshape(values.shape)
    return (layer_out, weight_grad, query_grad, key_grad, value_grad)
```

```python
import functools

import jax
import jax.numpy as jnp
from jax import lax
from jax.experimental import pallas as pl
from jax.experimental.pallas import tpu as pltpu
from jax.sharding import PartitionSpec as P

BF = jnp.bfloat16
F32 = jnp.float32
MESH = pl.DeviceIdType.MESH
MASKED = -1e30
GRIDS = {64: (4, 8), 8: (2, 2)}

NN = (((1,), (0,)), ((), ()))
NT = (((1,), (1,)), ((), ()))
TN = (((0,), (0,)), ((), ()))


def dot(a, b, dims=NN):
    return lax.dot_general(a, b, dims, preferred_element_type=F32)


def eye(n):
    rows = lax.broadcasted_iota(jnp.int32, (n, n), 0)
    cols = lax.broadcasted_iota(jnp.int32, (n, n), 1)
    return jnp.where(rows == cols, 1.0, 0.0).astype(BF)


def block_diagonal(pair):
    zero = jnp.zeros((64, pair.shape[1]), pair.dtype)
    first = jnp.concatenate([pair[:64], zero], axis=0)
    second = jnp.concatenate([zero, pair[64:]], axis=0)
    return jnp.concatenate([first, second], axis=1)


class Wires:
    def __init__(self, send_sems, recv_sems):
        self.send_sems, self.recv_sems = send_sems, recv_sems
        self.count = 0
        self.sent = []

    def send(self, src, dst, device_id):
        copy = pltpu.make_async_remote_copy(
            src_ref=src,
            dst_ref=dst,
            send_sem=self.send_sems.at[self.count],
            recv_sem=self.recv_sems.at[self.count],
            device_id=device_id,
            device_id_type=MESH,
        )
        self.count += 1
        copy.start()
        self.sent.append(copy)
        return copy

    def finish(self):
        for copy in self.sent:
            copy.wait_send()


def layer_kernel(
    dims,
    q_ref, k_hbm, v_hbm, len_ref, w_ref, g_ref,
    lo_ref, wg_ref, dq_ref, dk_hbm, dv_hbm,
    kb, vb, dkb, dvb, pb, bias,
    qb, gb, cb, fgb, dots,
    po, st, rco, rcs, tbo, tbs, ryo, rys, tzo, tzs, rzo, rzs, sg,
    pg, rcg, tbg, ryg, tzg, rzg,
    pd, rcd, tbd, ryd, tzd, rzd,
    wgp, rxw, wgf,
    send_sems, recv_sems, load_sems, store_sems,
):
    X, Y, Z, tokens = dims
    heads = Y * Z
    keys = kb.shape[0]
    width = Z * 64
    x = lax.axis_index("dp")
    me = lax.axis_index("psg")
    c = lax.rem(me, 2)
    chip = me // 2
    z = lax.rem(chip, Z)
    y = chip // Z

    def at_z(k):
        return {"psg": (y * Z + lax.rem(z + k, Z)) * 2 + c}

    def at_y(k):
        return {"psg": (lax.rem(y + k, Y) * Z + z) * 2 + c}

    def at_x(k):
        return {"dp": lax.rem(x + k, X)}

    partner = {"psg": chip * 2 + (1 - c)}
    wires = Wires(send_sems, recv_sems)

    def block_of(k):
        return lax.rem(y + k, Y)

    def rows(b):
        return pl.ds(b * Z, Z)

    def lanes(b):
        return pl.ds(pl.multiple_of(b * width, width), width)

    loads = []
    for i in range(Y):
        b = block_of(i + 1)
        pair = []
        for n, (src, dst) in enumerate(((k_hbm, kb), (v_hbm, vb))):
            copy = pltpu.make_async_copy(
                src.at[:, lanes(b)], dst.at[:, lanes(b)], load_sems.at[2 * i + n]
            )
            copy.start()
            pair.append(copy)
        loads.append(pair)

    barrier = pltpu.get_barrier_semaphore()
    peers = [partner]
    peers += [at_z(k) for k in range(1, Z)]
    peers += [at_y(k) for k in range(1, Y)]
    peers += [at_x(k) for k in range(1, X)]
    for peer in peers:
        pl.semaphore_signal(barrier, inc=1, device_id=peer, device_id_type=MESH)

    qb[chip, c] = dot(eye(32), q_ref[...], NT).astype(BF)
    g_t = dot(eye(64), g_ref[...], NT).astype(BF)
    pl.semaphore_wait(barrier, len(peers))

    def gather_z(buf):
        return [wires.send(buf.at[chip, c], buf.at[chip, c], at_z(k)) for k in range(1, Z)]

    def gather_y(buf, z_copies):
        for copy in z_copies:
            copy.wait_recv()
        own = buf.at[rows(y), c]
        y_copies = [wires.send(own, own, at_y(k)) for k in range(1, Y)]
        return y_copies, [wires.send(own, own, partner)]

    def gather_core(buf, y_copies, core_copies):
        core_copies = list(core_copies)
        for k in range(1, Y):
            y_copies[k - 1].wait_recv()
            part = buf.at[rows(block_of(Y - k)), c]
            core_copies.append(wires.send(part, part, partner))
        return core_copies

    def gather_end(core_copies):
        for copy in core_copies:
            copy.wait_recv()

    def scatter_core(part, landing, b):
        return wires.send(part.at[rows(b), 1 - c], landing.at[rows(b)], partner)

    def scatter_y(part, landing, total, landing_y, copy, b, k):
        copy.wait_recv()
        both = part[rows(b), c].astype(F32) + landing[rows(b)].astype(F32)
        total[rows(b)] = both.astype(BF)
        if k < Y:
            return wires.send(total.at[rows(b)], landing_y.at[k - 1], at_y(k))
        return None

    def scatter_z(total, landing_y, total_z, landing_z, copies):
        both = total[rows(y)].astype(F32)
        for k in range(1, Y):
            copies[k - 1].wait_recv()
            both = both + landing_y[k - 1].astype(F32)
        total_z[...] = both.astype(BF)
        return [
            wires.send(total_z.at[lax.rem(z + k, Z)], landing_z.at[k - 1], at_z(k))
            for k in range(1, Z)
        ]

    def scatter_end(total_z, landing_z, copies):
        both = total_z[z].astype(F32)
        for k in range(1, Z):
            copies[k - 1].wait_recv()
            both = both + landing_z[k - 1].astype(F32)
        return both

    q_z = gather_z(qb)
    g_core = []
    for i in range(Y):
        b = block_of(i + 1)
        term = dot(w_ref[:, lanes(b)], g_t, TN)
        pg[rows(b)] = term.reshape(Z, 2, 32, term.shape[1]).astype(BF)
        g_core.append(scatter_core(pg, rcg, b))
    q_y, q_core = gather_y(qb, q_z)
    g_y = []
    for i in range(Y):
        g_y.append(scatter_y(pg, rcg, tbg, ryg, g_core[i], block_of(i + 1), i + 1))

    for passage in range(keys // tokens):
        position = lax.broadcasted_iota(jnp.int32, (tokens, bias.shape[1]), 0)
        bias[passage * tokens : (passage + 1) * tokens] = jnp.where(
            position < len_ref[0, passage], 0.0, MASKED
        )
    q_core = gather_core(qb, q_y, q_core)
    g_z = scatter_z(tbg, ryg, tzg, rzg, g_y)
    gather_end(q_core)

    def forward_pair(j):
        columns = pl.ds(pl.multiple_of(j * 128, 128), 128)
        answers = qb.shape[3]
        query = block_diagonal(qb[pl.ds(2 * j, 2)].reshape(128, answers))
        scores = dot(kb[:, columns], query)
        for half in range(2):
            part = scores[:, half * answers : (half + 1) * answers] + bias[...]
            top = jnp.max(part, axis=0, keepdims=True)
            weights = jnp.exp(part - top)
            st[2 * j + half, 0:1, :] = top
            st[2 * j + half, 1:2, :] = jnp.sum(weights, axis=0, keepdims=True)
            pb[j, :, half * answers : (half + 1) * answers] = weights.astype(BF)
        out = dot(vb[:, columns], pb[j], TN)
        po[2 * j] = out[:64, :answers].reshape(2, 32, answers).astype(BF)
        po[2 * j + 1] = out[64:, answers:].reshape(2, 32, answers).astype(BF)

    def run_block(body, b):
        @pl.loop(0, Z // 2)
        def _(i):
            body(b * (Z // 2) + i)

    def merge(terms):
        top = terms[0][1]
        for _, other, _ in terms[1:]:
            top = jnp.maximum(top, other)
        output, total = None, None
        for out, own, part in terms:
            scale = jnp.exp(own - top)
            output = out * scale if output is None else output + out * scale
            total = part * scale if total is None else total + part * scale
        return output, top, total

    def triple(out, stats):
        return out.astype(F32), stats[..., 0:1, :], stats[..., 1:2, :]

    def output_core(b):
        return scatter_core(po, rco, b), wires.send(st.at[rows(b)], rcs.at[rows(b)], partner)

    def output_y(copies, b, k):
        for copy in copies:
            copy.wait_recv()
        output, top, total = merge(
            [triple(po[rows(b), c], st[rows(b)]), triple(rco[rows(b)], rcs[rows(b)])]
        )
        tbo[rows(b)] = output.astype(BF)
        tbs[rows(b), 0:1, :] = top
        tbs[rows(b), 1:2, :] = total
        if k == Y:
            return None
        return (
            wires.send(tbo.at[rows(b)], ryo.at[k - 1], at_y(k)),
            wires.send(tbs.at[rows(b)], rys.at[k - 1], at_y(k)),
        )

    o_core, o_y = [], []
    for i in range(Y):
        b = block_of(i + 1)
        for copy in loads[i]:
            copy.wait()
        run_block(forward_pair, b)
        o_core.append(output_core(b))
        if i > 0:
            o_y.append(output_y(o_core[i - 1], block_of(i), i))
        if i == 0:
            gb[chip, c] = scatter_end(tzg, rzg, g_z).astype(BF)
            gg_z = gather_z(gb)
        if i == 1:
            gg_y, gg_core = gather_y(gb, gg_z)
    output_y(o_core[Y - 1], y, Y)
    gg_core = gather_core(gb, gg_y, gg_core)

    terms = [triple(tbo[rows(y)], tbs[rows(y)])]
    for k in range(1, Y):
        for copy in o_y[k - 1]:
            copy.wait_recv()
        terms.append(triple(ryo[k - 1], rys[k - 1]))
    output, top, total = merge(terms)
    tzo[...] = output.astype(BF)
    tzs[:, 0:1, :] = top
    tzs[:, 1:2, :] = total
    o_z = []
    for k in range(1, Z):
        t = lax.rem(z + k, Z)
        o_z.append(
            (
                wires.send(tzo.at[t], rzo.at[k - 1], at_z(k)),
                wires.send(tzs.at[t], rzs.at[k - 1], at_z(k)),
            )
        )
    terms = [triple(tzo[z], tzs[z])]
    for k in range(1, Z):
        for copy in o_z[k - 1]:
            copy.wait_recv()
        terms.append(triple(rzo[k - 1], rzs[k - 1]))
    output, top, total = merge(terms)
    context = (output / total).astype(BF)
    cb[chip, c] = context
    sg[chip, c, 0:1, :] = top
    sg[chip, c, 1:2, :] = total
    sg[chip, c, 2:3, :] = jnp.sum(
        gb[chip, c].astype(F32) * context.astype(F32), axis=0, keepdims=True
    )
    sg[chip, c, 3:4, :] = total

    s_z = gather_z(sg)
    c_z = gather_z(cb)
    s_y, s_core = gather_y(sg, s_z)
    c_y, c_core = gather_y(cb, c_z)
    s_core = gather_core(sg, s_y, s_core)
    gather_end(gg_core)
    gather_end(s_core)

    for b in range(Y):
        part = slice(b * Z, (b + 1) * Z)
        factor = jnp.exp(st[part, 0:1, :] - sg[part, 0, 0:1, :]) / sg[part, 0, 1:2, :]
        dots[part] = factor * (sg[part, 0, 2:3, :] + sg[part, 1, 2:3, :])
        grads = gb[part].astype(F32).reshape(Z, 64, gb.shape[3]) * factor
        fgb[part] = grads.astype(BF).reshape(Z, 2, 32, gb.shape[3])

    def backward_pair(j):
        columns = pl.ds(pl.multiple_of(j * 128, 128), 128)
        answers = qb.shape[3]
        query = block_diagonal(qb[pl.ds(2 * j, 2)].reshape(128, answers))
        grad = block_diagonal(fgb[pl.ds(2 * j, 2)].reshape(128, answers))
        row_dots = jnp.concatenate([dots[2 * j], dots[2 * j + 1]], axis=1)
        weight_grad = dot(vb[:, columns], grad)
        weights = pb[j]
        score_grad = (weights.astype(F32) * (weight_grad - row_dots)).astype(BF)
        dvb[:, columns] = dot(weights, grad, NT).astype(BF)
        dkb[:, columns] = dot(score_grad, query, NT).astype(BF)
        out = dot(kb[:, columns], score_grad, TN)
        pd[2 * j] = out[:64, :answers].reshape(2, 32, answers).astype(BF)
        pd[2 * j + 1] = out[64:, answers:].reshape(2, 32, answers).astype(BF)

    d_core, d_y, stores = [], [], []
    for i in range(Y):
        b = block_of(i + 1)
        run_block(backward_pair, b)
        d_core.append(scatter_core(pd, rcd, b))
        for n, (src, dst) in enumerate(((dkb, dk_hbm), (dvb, dv_hbm))):
            copy = pltpu.make_async_copy(
                src.at[:, lanes(b)], dst.at[:, lanes(b)], store_sems.at[2 * i + n]
            )
            copy.start()
            stores.append(copy)
        if i > 0:
            d_y.append(scatter_y(pd, rcd, tbd, ryd, d_core[i - 1], block_of(i), i))
        if i == 0:
            c_core = gather_core(cb, c_y, c_core)
        if i == 1:
            gather_end(c_core)
            everything = cb[...].reshape(heads * 64, cb.shape[3])
            out_t = dot(w_ref[...], everything).astype(BF)
            lo_ref[...] = dot(eye(out_t.shape[1]), out_t, NT).astype(BF)
            span = heads * 64 // X
            for n in range(X):
                wgp[n] = dot(g_t, everything[n * span : (n + 1) * span], NT).astype(BF)
            w_copies = [
                wires.send(wgp.at[lax.rem(x + k, X)], rxw.at[k - 1], at_x(k)) for k in range(1, X)
            ]
        if i == min(2, Y - 1):
            both = wgp[x].astype(F32)
            for k in range(1, X):
                w_copies[k - 1].wait_recv()
                both = both + rxw[k - 1].astype(F32)
            wgf[x] = both.astype(BF)
            w_copies = [wires.send(wgf.at[x], wgf.at[x], at_x(k)) for k in range(1, X)]
    scatter_y(pd, rcd, tbd, ryd, d_core[Y - 1], y, Y)
    d_z = scatter_z(tbd, ryd, tzd, rzd, d_y)
    for copy in w_copies:
        copy.wait_recv()
    span = heads * 64 // X
    for n in range(X):
        wg_ref[:, n * span : (n + 1) * span] = wgf[n]
    own = scatter_end(tzd, rzd, d_z).astype(BF)
    dq_ref[...] = dot(eye(own.shape[1]), own, NT).astype(BF)

    for copy in stores:
        copy.wait()
    wires.finish()


def per_device(grid, chips_x, queries, keys, values, lengths, out_weight, out_cotangent):
    Y, Z = grid
    X = chips_x
    answers = queries.shape[1]
    tokens = keys.shape[2]
    count = keys.shape[1] * tokens
    inner = keys.shape[3]
    heads = inner // 64
    model = out_weight.shape[0]
    span = inner // X
    vmem = pltpu.VMEM

    def reduce_buffers():
        return [
            vmem((heads, 2, 32, answers), BF),
            vmem((heads, 32, answers), BF),
            vmem((heads, 32, answers), BF),
            vmem((Y - 1, Z, 32, answers), BF),
            vmem((Z, 32, answers), BF),
            vmem((Z - 1, 32, answers), BF),
        ]

    full = vmem((heads, 2, 32, answers), BF)
    scratch = [
        vmem((count, inner), BF),
        vmem((count, inner), BF),
        vmem((count, inner), BF),
        vmem((count, inner), BF),
        vmem((heads // 2, count, 2 * answers), BF),
        vmem((count, answers), F32),
        full, full, full, full,
        vmem((heads, 1, answers), F32),
        vmem((heads, 2, 32, answers), BF),
        vmem((heads, 2, answers), F32),
        vmem((heads, 32, answers), BF),
        vmem((heads, 2, answers), F32),
        vmem((heads, 32, answers), BF),
        vmem((heads, 2, answers), F32),
        vmem((Y - 1, Z, 32, answers), BF),
        vmem((Y - 1, Z, 2, answers), F32),
        vmem((Z, 32, answers), BF),
        vmem((Z, 2, answers), F32),
        vmem((Z - 1, 32, answers), BF),
        vmem((Z - 1, 2, answers), F32),
        vmem((heads, 2, 4, answers), F32),
        *reduce_buffers(),
        *reduce_buffers(),
        vmem((X, model, span), BF),
        vmem((X - 1, model, span), BF),
        vmem((X, model, span), BF),
    ]
    gather = (Z - 1) + (Y - 1) + Y
    scatter = Y + (Y - 1) + (Z - 1)
    copies = 4 * gather + 4 * scatter + 2 * (X - 1)
    scratch += [
        pltpu.SemaphoreType.DMA((copies,)),
        pltpu.SemaphoreType.DMA((copies,)),
        pltpu.SemaphoreType.DMA((2 * Y,)),
        pltpu.SemaphoreType.DMA((2 * Y,)),
    ]
    in_vmem = pl.BlockSpec(memory_space=pltpu.VMEM)
    in_place = pl.BlockSpec(memory_space=pl.ANY)
    layer_out, weight_grad, query_grad, key_grad, value_grad = pl.pallas_call(
        functools.partial(layer_kernel, (X, Y, Z, tokens)),
        out_shape=(
            jax.ShapeDtypeStruct((answers, model), BF),
            jax.ShapeDtypeStruct((model, inner), BF),
            jax.ShapeDtypeStruct((answers, queries.shape[2]), BF),
            jax.ShapeDtypeStruct((count, inner), BF),
            jax.ShapeDtypeStruct((count, inner), BF),
        ),
        in_specs=[
            in_vmem, in_place, in_place,
            pl.BlockSpec(memory_space=pltpu.SMEM),
            in_vmem, in_vmem,
        ],
        out_specs=(in_vmem, in_vmem, in_vmem, in_place, in_place),
        scratch_shapes=scratch,
        compiler_params=pltpu.CompilerParams(
            collective_id=0, has_side_effects=True, vmem_limit_bytes=56 << 20
        ),
    )(
        queries[0],
        keys.reshape(count, inner),
        values.reshape(count, inner),
        lengths,
        out_weight,
        out_cotangent[0],
    )
    return (
        layer_out[None],
        weight_grad.astype(F32),
        query_grad[None],
        key_grad.reshape(keys.shape),
        value_grad.reshape(values.shape),
    )


def solution(mesh):
    body = functools.partial(per_device, GRIDS[mesh.shape["psg"]], mesh.shape["dp"])
    return jax.shard_map(
        body,
        mesh=mesh,
        in_specs=(
            P("dp", None, "psg"),
            P("dp", "psg", None, None),
            P("dp", "psg", None, None),
            P("dp", "psg"),
            P("psg", None),
            P("dp", None, "psg"),
        ),
        out_specs=(
            P("dp", None, "psg"),
            P("psg", None),
            P("dp", None, "psg"),
            P("dp", "psg", None, None),
            P("dp", "psg", None, None),
        ),
        check_vma=False,
    )
```

```python
import functools

import jax
import jax.numpy as jnp
from jax import lax
from jax.experimental import pallas as pl
from jax.experimental.pallas import tpu as pltpu
from jax.sharding import PartitionSpec as P

BF = jnp.bfloat16
F32 = jnp.float32
MESH = pl.DeviceIdType.MESH
MASKED = -1e30
GRIDS = {64: (4, 8), 8: (2, 2)}

NN = (((1,), (0,)), ((), ()))
NT = (((1,), (1,)), ((), ()))
TN = (((0,), (0,)), ((), ()))


def dot(a, b, dims=NN):
    return lax.dot_general(a, b, dims, preferred_element_type=F32)


def block_diagonal(pair):
    zero = jnp.zeros((64, pair.shape[1]), pair.dtype)
    first = jnp.concatenate([pair[:64], zero], axis=0)
    second = jnp.concatenate([zero, pair[64:]], axis=0)
    return jnp.concatenate([first, second], axis=1)


class Wires:
    def __init__(self, send_sems, recv_sems):
        self.send_sems, self.recv_sems = send_sems, recv_sems
        self.count = 0
        self.sent = []

    def send(self, src, dst, device_id):
        copy = pltpu.make_async_remote_copy(
            src_ref=src,
            dst_ref=dst,
            send_sem=self.send_sems.at[self.count],
            recv_sem=self.recv_sems.at[self.count],
            device_id=device_id,
            device_id_type=MESH,
        )
        self.count += 1
        copy.start()
        self.sent.append(copy)
        return copy

    def finish(self):
        for copy in self.sent:
            copy.wait_send()


def layer_kernel(
    dims,
    q_hbm, k_hbm, v_hbm, len_ref, w_hbm, g_hbm,
    lo_ref, wg_ref, dq_ref, dkb, dvb,
    w_ref, g_ref, kb, vb, pb, ub, bias,
    qb, gb, cb, fgb, fqb, fdb, ab, bb, cen,
    po, st, rco, rcs, tbo, tbs, ryo, rys, tzo, tzs, rzo, rzs, sg,
    pg, rcg, tbg, ryg, tzg, rzg,
    pd, rcd, tbd, ryd, tzd, rzd,
    wgp, rxw, wgf,
    send_sems, recv_sems, load_sems,
):
    X, Y, Z, tokens = dims
    heads = Y * Z
    keys = kb.shape[0]
    answers = qb.shape[3]
    width = Z * 64
    x = lax.axis_index("dp")
    me = lax.axis_index("psg")
    c = lax.rem(me, 2)
    chip = me // 2
    z = lax.rem(chip, Z)
    y = chip // Z

    def at_yz(dy, dz):
        return {"psg": (lax.rem(y + dy, Y) * Z + lax.rem(z + dz, Z)) * 2 + c}

    def at_z(k):
        return at_yz(0, k)

    def at_y(k):
        return at_yz(k, 0)

    def at_x(k):
        return {"dp": lax.rem(x + k, X)}

    def hops(dy, dz):
        return min(dy, Y - dy) + min(dz, Z - dz)

    far_first = sorted(
        [(dy, dz) for dy in range(Y) for dz in range(Z) if (dy, dz) != (0, 0)],
        key=lambda d: -hops(*d),
    )
    near_rows = sorted(range(Y), key=lambda dy: min(dy, Y - dy))
    partner = {"psg": chip * 2 + (1 - c)}
    wires = Wires(send_sems, recv_sems)

    def block_of(k):
        return lax.rem(y + k, Y)

    def rows(b):
        return pl.ds(b * Z, Z)

    def lanes(b):
        return pl.ds(pl.multiple_of(b * width, width), width)

    barrier = pltpu.get_barrier_semaphore()
    peers = [at_yz(*d) for d in far_first] + [partner] + [at_x(k) for k in range(1, X)]
    for peer in peers:
        pl.semaphore_signal(barrier, inc=1, device_id=peer, device_id_type=MESH)

    small = []
    for n, (src, dst) in enumerate(((q_hbm, qb.at[chip, c]), (g_hbm, g_ref), (w_hbm, w_ref))):
        copy = pltpu.make_async_copy(src, dst, load_sems.at[2 * Y + n])
        copy.start()
        small.append(copy)
    loads = []
    for i in range(Y):
        b = block_of(i + 1)
        pair = []
        for n, (src, dst) in enumerate(((k_hbm, kb), (v_hbm, vb))):
            copy = pltpu.make_async_copy(
                src.at[:, lanes(b)], dst.at[:, lanes(b)], load_sems.at[2 * i + n]
            )
            copy.start()
            pair.append(copy)
        loads.append(pair)
    for copy in small:
        copy.wait()
    g_t = g_ref[...]
    pl.semaphore_wait(barrier, len(peers))

    def gather_start(buf):
        own = buf.at[chip, c]
        return {d: wires.send(own, own, at_yz(*d)) for d in far_first}

    def gather_core(buf, copies):
        core_copies = []
        for dy in near_rows:
            for dz in range(Z):
                if (dy, dz) in copies:
                    copies[dy, dz].wait_recv()
            part = buf.at[rows(block_of(Y - dy)), c]
            core_copies.append(wires.send(part, part, partner))
        return core_copies

    def gather_end(core_copies):
        for copy in core_copies:
            copy.wait_recv()

    def scatter_core(part, landing, b):
        return wires.send(part.at[rows(b), 1 - c], landing.at[rows(b)], partner)

    def scatter_y(part, landing, total, landing_y, copy, b, k):
        copy.wait_recv()
        both = part[rows(b), c].astype(F32) + landing[rows(b)].astype(F32)
        total[rows(b)] = both.astype(BF)
        if k < Y:
            return wires.send(total.at[rows(b)], landing_y.at[k - 1], at_y(k))
        return None

    def scatter_z(total, landing_y, total_z, landing_z, copies):
        both = total[rows(y)].astype(F32)
        for k in range(1, Y):
            copies[k - 1].wait_recv()
            both = both + landing_y[k - 1].astype(F32)
        total_z[...] = both.astype(BF)
        return [
            wires.send(total_z.at[lax.rem(z + k, Z)], landing_z.at[k - 1], at_z(k))
            for k in range(1, Z)
        ]

    def scatter_end(total_z, landing_z, copies):
        both = total_z[z].astype(F32)
        for k in range(1, Z):
            copies[k - 1].wait_recv()
            both = both + landing_z[k - 1].astype(F32)
        return both

    q_copies = gather_start(qb)
    g_core = []
    for i in range(Y):
        b = block_of(i + 1)
        term = dot(w_ref[:, lanes(b)], g_t, TN)
        pg[rows(b)] = term.reshape(Z, 2, 32, answers).astype(BF)
        g_core.append(scatter_core(pg, rcg, b))
    for passage in range(keys // tokens):
        position = lax.broadcasted_iota(jnp.int32, (tokens, answers), 0)
        bias[passage * tokens : (passage + 1) * tokens] = jnp.where(
            position < len_ref[0, passage], 0.0, MASKED
        )
    g_y = []
    for i in range(Y):
        g_y.append(scatter_y(pg, rcg, tbg, ryg, g_core[i], block_of(i + 1), i + 1))
    q_core = gather_core(qb, q_copies)
    g_z = scatter_z(tbg, ryg, tzg, rzg, g_y)
    gather_end(q_core)

    def columns(j):
        return pl.ds(pl.multiple_of(j * 128, 128), 128)

    def pair_of(buf, j):
        return block_diagonal(buf[pl.ds(2 * j, 2)].reshape(128, answers))

    def forward_pair(j):
        scores = dot(kb[:, columns(j)], pair_of(qb, j))
        for half in range(2):
            part = scores[:, half * answers : (half + 1) * answers] + bias[...]
            top = jnp.max(part, axis=0, keepdims=True)
            weights = jnp.exp(part - top)
            st[2 * j + half, 0:1, :] = top
            st[2 * j + half, 1:2, :] = jnp.sum(weights, axis=0, keepdims=True)
            pb[j, :, half * answers : (half + 1) * answers] = weights.astype(BF)
        out = dot(vb[:, columns(j)], pb[j], TN)
        po[2 * j] = out[:64, :answers].reshape(2, 32, answers).astype(BF)
        po[2 * j + 1] = out[64:, answers:].reshape(2, 32, answers).astype(BF)

    def run_block(body, b):
        @pl.loop(0, Z // 2)
        def _(i):
            body(b * (Z // 2) + i)

    def merge(terms):
        top = terms[0][1]
        for _, other, _ in terms[1:]:
            top = jnp.maximum(top, other)
        output, total = None, None
        for out, own, part in terms:
            scale = jnp.exp(own - top)
            output = out * scale if output is None else output + out * scale
            total = part * scale if total is None else total + part * scale
        return output, top, total

    def triple(out, stats):
        return out.astype(F32), stats[..., 0:1, :], stats[..., 1:2, :]

    def output_core(b):
        return scatter_core(po, rco, b), wires.send(st.at[rows(b)], rcs.at[rows(b)], partner)

    def output_y(copies, b, k):
        for copy in copies:
            copy.wait_recv()
        output, top, total = merge(
            [triple(po[rows(b), c], st[rows(b)]), triple(rco[rows(b)], rcs[rows(b)])]
        )
        tbo[rows(b)] = output.astype(BF)
        tbs[rows(b), 0:1, :] = top
        tbs[rows(b), 1:2, :] = total
        if k == Y:
            return None
        return (
            wires.send(tbo.at[rows(b)], ryo.at[k - 1], at_y(k)),
            wires.send(tbs.at[rows(b)], rys.at[k - 1], at_y(k)),
        )

    def output_z():
        terms = [triple(tbo[rows(y)], tbs[rows(y)])]
        for k in range(1, Y):
            for copy in o_y[k - 1]:
                copy.wait_recv()
            terms.append(triple(ryo[k - 1], rys[k - 1]))
        output, top, total = merge(terms)
        tzo[...] = output.astype(BF)
        tzs[:, 0:1, :] = top
        tzs[:, 1:2, :] = total
        copies = []
        for k in range(1, Z):
            t = lax.rem(z + k, Z)
            copies.append(
                (
                    wires.send(tzo.at[t], rzo.at[k - 1], at_z(k)),
                    wires.send(tzs.at[t], rzs.at[k - 1], at_z(k)),
                )
            )
        return copies

    def output_end(copies):
        terms = [triple(tzo[z], tzs[z])]
        for k in range(1, Z):
            for copy in copies[k - 1]:
                copy.wait_recv()
            terms.append(triple(rzo[k - 1], rzs[k - 1]))
        return merge(terms)

    def middle_pair(j):
        centers = []
        for half in range(2):
            h = 2 * j + half
            products = gb[h].astype(F32) * po[h].astype(F32)
            center = jnp.sum(products.reshape(64, answers), axis=0, keepdims=True) / st[h, 1:2, :]
            cen[h] = center
            centers.append(center)
        prob_grad = dot(vb[:, columns(j)], pair_of(gb, j))
        weights = pb[j]
        centered = prob_grad - jnp.concatenate(centers, axis=1)
        score_grad = (weights.astype(F32) * centered).astype(BF)
        ub[j] = score_grad
        key_pair = kb[:, columns(j)]
        for out, terms in ((ab, score_grad), (bb, weights)):
            product = dot(key_pair, terms, TN)
            out[2 * j] = product[:64, :answers]
            out[2 * j + 1] = product[64:, answers:]

    o_core, o_y = [], []
    for i in range(Y):
        b = block_of(i + 1)
        for copy in loads[i]:
            copy.wait()
        run_block(forward_pair, b)
        o_core.append(output_core(b))
        if i > 0:
            o_y.append(output_y(o_core[i - 1], block_of(i), i))
        if i == 0:
            gb[chip, c] = scatter_end(tzg, rzg, g_z).astype(BF)
            g_copies = gather_start(gb)
    output_y(o_core[Y - 1], y, Y)
    o_z = output_z()
    gather_end(gather_core(gb, g_copies))
    for b in range(Y - 1):
        run_block(middle_pair, b)

    output, top, total = output_end(o_z)
    context = (output / total).astype(BF)
    cb[chip, c] = context
    sg[chip, c, 0:1, :] = top
    sg[chip, c, 1:2, :] = total
    sg[chip, c, 2:3, :] = jnp.sum(
        gb[chip, c].astype(F32) * context.astype(F32), axis=0, keepdims=True
    )
    sg[chip, c, 3:4, :] = total
    s_copies = gather_start(sg)
    c_copies = gather_start(cb)
    run_block(middle_pair, Y - 1)
    s_core = gather_core(sg, s_copies)
    gather_end(s_core)

    d_core = []
    for i in range(Y):
        b = block_of(i + 1)
        stats = sg[rows(b)]
        factor = jnp.exp(st[rows(b), 0:1, :] - stats[:, 0, 0:1, :]) / stats[:, 0, 1:2, :]
        shift = factor * (stats[:, 0, 2:3, :] + stats[:, 1, 2:3, :] - cen[rows(b)])
        query_terms = factor * ab[rows(b)] - shift * bb[rows(b)]
        pd[rows(b)] = query_terms.astype(BF).reshape(Z, 2, 32, answers)
        d_core.append(scatter_core(pd, rcd, b))

        def scaled(buf, by):
            wide = buf[rows(b)].astype(F32).reshape(Z, 64, answers) * by
            return wide.astype(BF).reshape(Z, 2, 32, answers)

        fgb[rows(b)] = scaled(gb, factor)
        fqb[rows(b)] = scaled(qb, factor)
        fdb[rows(b)] = scaled(qb, -shift)

    def backward_pair(j):
        both = jnp.concatenate([pair_of(fgb, j), pair_of(fdb, j)], axis=0)
        from_weights = dot(pb[j], both, NT)
        dvb[:, columns(j)] = from_weights[:, :128].astype(BF)
        key_grad = from_weights[:, 128:] + dot(ub[j], pair_of(fqb, j), NT)
        dkb[:, columns(j)] = key_grad.astype(BF)

    span = heads * 64 // X
    d_y = []
    for i in range(Y):
        d_y.append(scatter_y(pd, rcd, tbd, ryd, d_core[i], block_of(i + 1), i + 1))
    c_core = gather_core(cb, c_copies)
    run_block(backward_pair, 0)
    gather_end(c_core)
    everything = cb[...].reshape(heads * 64, answers)
    for n in range(X):
        wgp[n] = dot(g_t, everything[n * span : (n + 1) * span], NT).astype(BF)
    w_copies = [
        wires.send(wgp.at[lax.rem(x + k, X)], rxw.at[k - 1], at_x(k)) for k in range(1, X)
    ]
    d_z = scatter_z(tbd, ryd, tzd, rzd, d_y)
    lo_ref[...] = dot(w_ref[...], everything).astype(BF)
    for b in range(1, Y - 1):
        run_block(backward_pair, b)
    both = wgp[x].astype(F32)
    for k in range(1, X):
        w_copies[k - 1].wait_recv()
        both = both + rxw[k - 1].astype(F32)
    wgf[x] = both.astype(BF)
    w_copies = [wires.send(wgf.at[x], wgf.at[x], at_x(k)) for k in range(1, X)]
    run_block(backward_pair, Y - 1)
    dq_ref[...] = scatter_end(tzd, rzd, d_z).astype(BF)
    wires.finish()
    for copy in w_copies:
        copy.wait_recv()
    for n in range(X):
        wg_ref[:, n * span : (n + 1) * span] = wgf[n].astype(F32)


def store_kernel(*refs):
    count = (len(refs) - 1) // 2
    copies = [
        pltpu.make_async_copy(refs[n], refs[count + n], refs[-1].at[n]) for n in range(count)
    ]
    for copy in copies:
        copy.start()
    for copy in copies:
        copy.wait()


def per_device(grid, chips_x, queries, keys, values, lengths, out_weight, out_cotangent):
    Y, Z = grid
    X = chips_x
    answers = queries.shape[1]
    tokens = keys.shape[2]
    count = keys.shape[1] * tokens
    inner = keys.shape[3]
    heads = inner // 64
    model = out_weight.shape[0]
    span = inner // X
    vmem = pltpu.VMEM

    def reduce_buffers():
        return [
            vmem((heads, 2, 32, answers), BF),
            vmem((heads, 32, answers), BF),
            vmem((heads, 32, answers), BF),
            vmem((Y - 1, Z, 32, answers), BF),
            vmem((Z, 32, answers), BF),
            vmem((Z - 1, 32, answers), BF),
        ]

    full = vmem((heads, 2, 32, answers), BF)
    scratch = [
        vmem((model, inner), BF),
        vmem((model, answers), BF),
        vmem((count, inner), BF),
        vmem((count, inner), BF),
        vmem((heads // 2, count, 2 * answers), BF),
        vmem((heads // 2, count, 2 * answers), BF),
        vmem((count, answers), F32),
        full, full, full, full, full, full,
        vmem((heads, 64, answers), F32),
        vmem((heads, 64, answers), F32),
        vmem((heads, 1, answers), F32),
        vmem((heads, 2, 32, answers), BF),
        vmem((heads, 2, answers), F32),
        vmem((heads, 32, answers), BF),
        vmem((heads, 2, answers), F32),
        vmem((heads, 32, answers), BF),
        vmem((heads, 2, answers), F32),
        vmem((Y - 1, Z, 32, answers), BF),
        vmem((Y - 1, Z, 2, answers), F32),
        vmem((Z, 32, answers), BF),
        vmem((Z, 2, answers), F32),
        vmem((Z - 1, 32, answers), BF),
        vmem((Z - 1, 2, answers), F32),
        vmem((heads, 2, 4, answers), F32),
        *reduce_buffers(),
        *reduce_buffers(),
        vmem((X, model, span), BF),
        vmem((X - 1, model, span), BF),
        vmem((X, model, span), BF),
    ]
    gather = heads - 1 + Y
    scatter = Y + (Y - 1) + (Z - 1)
    copies = 4 * gather + 4 * scatter + 2 * (X - 1)
    scratch += [
        pltpu.SemaphoreType.DMA((copies,)),
        pltpu.SemaphoreType.DMA((copies,)),
        pltpu.SemaphoreType.DMA((2 * Y + 3,)),
    ]
    in_vmem = pl.BlockSpec(memory_space=pltpu.VMEM)
    in_hbm = pl.BlockSpec(memory_space=pltpu.HBM)
    shapes = (
        ((model, answers), BF),
        ((model, inner), F32),
        ((queries.shape[2], answers), BF),
        ((count, inner), BF),
        ((count, inner), BF),
    )
    results = pl.pallas_call(
        functools.partial(layer_kernel, (X, Y, Z, tokens)),
        out_shape=tuple(vmem(*shape) for shape in shapes),
        in_specs=[
            in_hbm, in_hbm, in_hbm,
            pl.BlockSpec(memory_space=pltpu.SMEM),
            in_hbm, in_hbm,
        ],
        out_specs=(in_vmem,) * len(shapes),
        scratch_shapes=scratch,
        compiler_params=pltpu.CompilerParams(
            collective_id=0, has_side_effects=True, vmem_limit_bytes=50 << 20
        ),
    )(
        queries[0].T,
        keys.reshape(count, inner),
        values.reshape(count, inner),
        lengths,
        out_weight,
        out_cotangent[0].T,
    )
    layer_out, weight_grad, query_grad, key_grad, value_grad = pl.pallas_call(
        store_kernel,
        out_shape=tuple(jax.ShapeDtypeStruct(*shape) for shape in shapes),
        in_specs=[in_vmem] * len(shapes),
        out_specs=(in_hbm,) * len(shapes),
        scratch_shapes=[pltpu.SemaphoreType.DMA((len(shapes),))],
        compiler_params=pltpu.CompilerParams(vmem_limit_bytes=4 << 20),
    )(*(pltpu.with_memory_space_constraint(part, pltpu.VMEM) for part in results))
    return (
        layer_out.T[None],
        weight_grad,
        query_grad.T[None],
        key_grad.reshape(keys.shape),
        value_grad.reshape(values.shape),
    )


def solution(mesh):
    body = functools.partial(per_device, GRIDS[mesh.shape["psg"]], mesh.shape["dp"])
    return jax.shard_map(
        body,
        mesh=mesh,
        in_specs=(
            P("dp", None, "psg"),
            P("dp", "psg", None, None),
            P("dp", "psg", None, None),
            P("dp", "psg"),
            P("psg", None),
            P("dp", None, "psg"),
        ),
        out_specs=(
            P("dp", None, "psg"),
            P("psg", None),
            P("dp", None, "psg"),
            P("dp", "psg", None, None),
            P("dp", "psg", None, None),
        ),
        check_vma=False,
    )
```

```python
import functools

import jax
import jax.numpy as jnp
from jax import lax
from jax.experimental import pallas as pl
from jax.experimental.pallas import tpu as pltpu
from jax.sharding import PartitionSpec as P

BF = jnp.bfloat16
F32 = jnp.float32
MESH = pl.DeviceIdType.MESH
MASKED = -1e30
GRIDS = {64: (4, 8), 8: (2, 2)}

NN = (((1,), (0,)), ((), ()))
NT = (((1,), (1,)), ((), ()))
TN = (((0,), (0,)), ((), ()))


def dot(a, b, dims=NN):
    return lax.dot_general(a, b, dims, preferred_element_type=F32)


def block_diagonal(pair):
    zero = jnp.zeros((64, pair.shape[1]), pair.dtype)
    first = jnp.concatenate([pair[:64], zero], axis=0)
    second = jnp.concatenate([zero, pair[64:]], axis=0)
    return jnp.concatenate([first, second], axis=1)


class Wires:
    def __init__(self, send_sems, recv_sems):
        self.send_sems, self.recv_sems = send_sems, recv_sems
        self.count = 0
        self.sent = []

    def send(self, src, dst, device_id):
        copy = pltpu.make_async_remote_copy(
            src_ref=src,
            dst_ref=dst,
            send_sem=self.send_sems.at[self.count],
            recv_sem=self.recv_sems.at[self.count],
            device_id=device_id,
            device_id_type=MESH,
        )
        self.count += 1
        copy.start()
        self.sent.append(copy)
        return copy

    def finish(self, keep=0):
        count = len(self.sent) - keep
        for copy in self.sent[:count]:
            copy.wait_send()
        self.sent = self.sent[count:]


def layer_kernel(
    dims,
    q_hbm, k_hbm, v_hbm, len_ref, w_hbm, g_hbm,
    lo_ref, wg_ref, dq_ref, dkb, dvb,
    w_ref, g_ref, kb, vb, pb, ub, bias,
    qb, gb, cb, fgb, fqb, fdb, ab, bb, cen,
    po, st, rco, rcs, tbo, tbs, ryo, rys, tzo, tzs, rzo, rzs, sg,
    pg, rcg, tbg, rzg,
    pd, rcd, tbd, rzd,
    wgp, rxw, wgf,
    send_sems, recv_sems, load_sems,
):
    X, Y, Z, tokens = dims
    heads = Y * Z
    keys = kb.shape[0]
    answers = qb.shape[3]
    width = Z * 64
    x = lax.axis_index("dp")
    me = lax.axis_index("psg")
    c = lax.rem(me, 2)
    chip = me // 2
    z = lax.rem(chip, Z)
    y = chip // Z

    def at_yz(dy, dz):
        return {"psg": (lax.rem(y + dy, Y) * Z + lax.rem(z + dz, Z)) * 2 + c}

    def at_z(k):
        return at_yz(0, k)

    def at_y(k):
        return at_yz(k, 0)

    def at_x(k):
        return {"dp": lax.rem(x + k, X)}

    targets = [
        (dy, dz)
        for dy in reversed(range(Y))
        for dz in sorted(range(Z), key=lambda dz: -min(dz, Z - dz))
        if (dy, dz) != (0, 0)
    ]
    partner = {"psg": chip * 2 + (1 - c)}
    wires = Wires(send_sems, recv_sems)

    def block_of(k):
        return lax.rem(y + k, Y)

    def rows(b):
        return pl.ds(b * Z, Z)

    def lanes(b):
        return pl.ds(pl.multiple_of(b * width, width), width)

    barrier = pltpu.get_barrier_semaphore()
    peers = [at_yz(*d) for d in targets] + [partner] + [at_x(k) for k in range(1, X)]
    for peer in peers:
        pl.semaphore_signal(barrier, inc=1, device_id=peer, device_id_type=MESH)

    small = []
    for n, (src, dst) in enumerate(((q_hbm, qb.at[chip, c]), (g_hbm, g_ref), (w_hbm, w_ref))):
        copy = pltpu.make_async_copy(src, dst, load_sems.at[2 * Y + n])
        copy.start()
        small.append(copy)
    loads = []
    for i in range(Y):
        b = block_of(i + 1)
        pair = []
        for n, (src, dst) in enumerate(((k_hbm, kb), (v_hbm, vb))):
            copy = pltpu.make_async_copy(
                src.at[:, lanes(b)], dst.at[:, lanes(b)], load_sems.at[2 * i + n]
            )
            copy.start()
            pair.append(copy)
        loads.append(pair)
    for copy in small:
        copy.wait()
    g_t = g_ref[...]
    pl.semaphore_wait(barrier, len(peers))

    def gather_start(buf):
        own = buf.at[chip, c]
        return {d: wires.send(own, own, at_yz(*d)) for d in targets}

    def gather_block(buf, copies, i):
        for dz in range(Z):
            if (Y - 1 - i, dz) in copies:
                copies[Y - 1 - i, dz].wait_recv()
        part = buf.at[rows(block_of(i + 1)), c]
        return wires.send(part, part, partner)

    def gather_core(buf, copies):
        return [gather_block(buf, copies, i) for i in range(Y)]

    def gather_end(core_copies):
        for copy in core_copies:
            copy.wait_recv()

    def scatter_core(part, landing, b):
        return wires.send(part.at[rows(b), 1 - c], landing.at[rows(b)], partner)

    def scatter_start(part, landing, total, pieces, core_copies):
        copies = []
        for i in range(Y):
            b = block_of(i + 1)
            core_copies[i].wait_recv()
            both = part[rows(b), c].astype(F32) + landing[rows(b)].astype(F32)
            total[rows(b)] = both.astype(BF)
            dy = (i + 1) % Y
            for dz in sorted(range(Z), key=lambda dz: -min(dz, Z - dz)):
                if (dy, dz) != (0, 0):
                    piece = total.at[b * Z + lax.rem(z + dz, Z)]
                    copies.append(
                        wires.send(piece, pieces.at[dy * Z + dz - 1], at_yz(dy, dz))
                    )
        return copies

    def scatter_end(total, pieces, copies):
        for copy in copies:
            copy.wait_recv()
        return total[chip].astype(F32) + jnp.sum(pieces[...].astype(F32), axis=0)

    q_copies = gather_start(qb)
    g_core = []
    for i in range(Y):
        b = block_of(i + 1)
        term = dot(w_ref[:, lanes(b)], g_t, TN)
        pg[rows(b)] = term.reshape(Z, 2, 32, answers).astype(BF)
        g_core.append(scatter_core(pg, rcg, b))
    for passage in range(keys // tokens):
        position = lax.broadcasted_iota(jnp.int32, (tokens, answers), 0)
        bias[passage * tokens : (passage + 1) * tokens] = jnp.where(
            position < len_ref[0, passage], 0.0, MASKED
        )
    g_pieces = scatter_start(pg, rcg, tbg, rzg, g_core)

    def columns(j):
        return pl.ds(pl.multiple_of(j * 128, 128), 128)

    def pair_of(buf, j):
        return block_diagonal(buf[pl.ds(2 * j, 2)].reshape(128, answers))

    def forward_pair(j):
        scores = dot(kb[:, columns(j)], pair_of(qb, j))
        for half in range(2):
            part = scores[:, half * answers : (half + 1) * answers] + bias[...]
            top = jnp.max(part, axis=0, keepdims=True)
            weights = jnp.exp(part - top)
            st[2 * j + half, 0:1, :] = top
            st[2 * j + half, 1:2, :] = jnp.sum(weights, axis=0, keepdims=True)
            pb[j, :, half * answers : (half + 1) * answers] = weights.astype(BF)
        out = dot(vb[:, columns(j)], pb[j], TN)
        po[2 * j] = out[:64, :answers].reshape(2, 32, answers).astype(BF)
        po[2 * j + 1] = out[64:, answers:].reshape(2, 32, answers).astype(BF)

    def run_block(body, b):
        @pl.loop(0, Z // 2, unroll=Z // 2)
        def _(i):
            body(b * (Z // 2) + i)

    def merge(terms):
        top = terms[0][1]
        for _, other, _ in terms[1:]:
            top = jnp.maximum(top, other)
        output, total = None, None
        for out, own, part in terms:
            scale = jnp.exp(own - top)
            output = out * scale if output is None else output + out * scale
            total = part * scale if total is None else total + part * scale
        return output, top, total

    def triple(out, stats):
        return out.astype(F32), stats[..., 0:1, :], stats[..., 1:2, :]

    def output_core(b):
        return scatter_core(po, rco, b), wires.send(st.at[rows(b)], rcs.at[rows(b)], partner)

    def output_y(copies, b, k):
        for copy in copies:
            copy.wait_recv()
        output, top, total = merge(
            [triple(po[rows(b), c], st[rows(b)]), triple(rco[rows(b)], rcs[rows(b)])]
        )
        tbo[rows(b)] = output.astype(BF)
        tbs[rows(b), 0:1, :] = top
        tbs[rows(b), 1:2, :] = total
        if k == Y:
            return None
        return (
            wires.send(tbo.at[rows(b)], ryo.at[k - 1], at_y(k)),
            wires.send(tbs.at[rows(b)], rys.at[k - 1], at_y(k)),
        )

    def output_z():
        terms = [triple(tbo[rows(y)], tbs[rows(y)])]
        for k in range(1, Y):
            for copy in o_y[k - 1]:
                copy.wait_recv()
            terms.append(triple(ryo[k - 1], rys[k - 1]))
        output, top, total = merge(terms)
        tzo[...] = output.astype(BF)
        tzs[:, 0:1, :] = top
        tzs[:, 1:2, :] = total
        copies = []
        for k in range(1, Z):
            t = lax.rem(z + k, Z)
            copies.append(
                (
                    wires.send(tzo.at[t], rzo.at[k - 1], at_z(k)),
                    wires.send(tzs.at[t], rzs.at[k - 1], at_z(k)),
                )
            )
        return copies

    def output_end(copies):
        terms = [triple(tzo[z], tzs[z])]
        for k in range(1, Z):
            for copy in copies[k - 1]:
                copy.wait_recv()
            terms.append(triple(rzo[k - 1], rzs[k - 1]))
        return merge(terms)

    def middle_pair(j):
        centers = []
        for half in range(2):
            h = 2 * j + half
            products = gb[h].astype(F32) * po[h].astype(F32)
            center = jnp.sum(products.reshape(64, answers), axis=0, keepdims=True) / st[h, 1:2, :]
            cen[h] = center
            centers.append(center)
        prob_grad = dot(vb[:, columns(j)], pair_of(gb, j))
        weights = pb[j]
        centered = prob_grad - jnp.concatenate(centers, axis=1)
        score_grad = (weights.astype(F32) * centered).astype(BF)
        ub[j] = score_grad
        key_pair = kb[:, columns(j)]
        for out, terms in ((ab, score_grad), (bb, weights)):
            product = dot(key_pair, terms, TN)
            out[2 * j] = product[:64, :answers]
            out[2 * j + 1] = product[64:, answers:]

    o_core, o_y = [], []
    q_core = [gather_block(qb, q_copies, 0)]
    for i in range(Y):
        b = block_of(i + 1)
        if i + 1 < Y:
            q_core.append(gather_block(qb, q_copies, i + 1))
        for copy in loads[i]:
            copy.wait()
        q_core[i].wait_recv()
        run_block(forward_pair, b)
        o_core.append(output_core(b))
        if i > 0:
            o_y.append(output_y(o_core[i - 1], block_of(i), i))
    output_y(o_core[Y - 1], y, Y)
    o_z = output_z()
    gb[chip, c] = scatter_end(tbg, rzg, g_pieces).astype(BF)
    g_copies = gather_start(gb)
    older = len(wires.sent)

    output, top, total = output_end(o_z)
    context = (output / total).astype(BF)
    cb[chip, c] = context
    sg[chip, c, 0:1, :] = top
    sg[chip, c, 1:2, :] = total
    sg[chip, c, 2:3, :] = jnp.sum(
        gb[chip, c].astype(F32) * context.astype(F32), axis=0, keepdims=True
    )
    sg[chip, c, 3:4, :] = total
    s_copies = gather_start(sg)
    c_copies = gather_start(cb)
    gather_end(gather_core(gb, g_copies))
    for b in range(Y):
        run_block(middle_pair, b)
    wires.finish(keep=len(wires.sent) - older)
    s_core = gather_core(sg, s_copies)
    gather_end(s_core)

    factors, shifts, d_core = [], [], []
    for i in range(Y):
        b = block_of(i + 1)
        stats = sg[rows(b)]
        factor = jnp.exp(st[rows(b), 0:1, :] - stats[:, 0, 0:1, :]) / stats[:, 0, 1:2, :]
        shift = factor * (stats[:, 0, 2:3, :] + stats[:, 1, 2:3, :] - cen[rows(b)])
        query_terms = factor * ab[rows(b)] - shift * bb[rows(b)]
        pd[rows(b)] = query_terms.astype(BF).reshape(Z, 2, 32, answers)
        d_core.append(scatter_core(pd, rcd, b))
        factors.append(factor)
        shifts.append(shift)

    c_core = gather_core(cb, c_copies)
    d_pieces = scatter_start(pd, rcd, tbd, rzd, d_core)

    span = width // X
    w_copies = []
    for i in range(Y):
        c_core[i].wait_recv()
        term = dot(g_t, cb[rows(block_of(i + 1))].reshape(width, answers), NT).astype(BF)
        for n in range(X):
            wgp[i, n] = term[:, n * span : (n + 1) * span]
        w_copies.append(
            [
                wires.send(wgp.at[i, lax.rem(x + k, X)], rxw.at[i, k - 1], at_x(k))
                for k in range(1, X)
            ]
        )

    for i in range(Y):
        b = block_of(i + 1)

        def scaled(buf, by):
            wide = buf[rows(b)].astype(F32).reshape(Z, 64, answers) * by
            return wide.astype(BF).reshape(Z, 2, 32, answers)

        fgb[rows(b)] = scaled(gb, factors[i])
        fqb[rows(b)] = scaled(qb, factors[i])
        fdb[rows(b)] = scaled(qb, -shifts[i])

    def backward_pair(j):
        both = jnp.concatenate([pair_of(fgb, j), pair_of(fdb, j)], axis=0)
        from_weights = dot(pb[j], both, NT)
        dvb[:, columns(j)] = from_weights[:, :128].astype(BF)
        key_grad = from_weights[:, 128:] + dot(ub[j], pair_of(fqb, j), NT)
        dkb[:, columns(j)] = key_grad.astype(BF)

    for b in range(Y // 2):
        run_block(backward_pair, b)
    sums = []
    for i in range(Y):
        b = block_of(i + 1)
        both = wgp[i, x].astype(F32)
        for k in range(1, X):
            w_copies[i][k - 1].wait_recv()
            both = both + rxw[i, k - 1].astype(F32)
        wgf[b, x] = both.astype(BF)
        sums += [wires.send(wgf.at[b, x], wgf.at[b, x], at_x(k)) for k in range(1, X)]
    for b in range(Y // 2, Y):
        run_block(backward_pair, b)
    lo_ref[...] = dot(w_ref[...], cb[...].reshape(heads * 64, answers)).astype(BF)
    wires.finish(keep=len(sums))
    dq_ref[...] = scatter_end(tbd, rzd, d_pieces).astype(BF)
    for copy in sums:
        copy.wait_recv()
    for b in range(Y):
        for n in range(X):
            at = (b * X + n) * span
            wg_ref[:, at : at + span] = wgf[b, n].astype(F32)
    wires.finish()


def store_kernel(*refs):
    count = (len(refs) - 1) // 2
    copies = [
        pltpu.make_async_copy(refs[n], refs[count + n], refs[-1].at[n]) for n in range(count)
    ]
    for copy in copies:
        copy.start()
    for copy in copies:
        copy.wait()


def per_device(grid, chips_x, queries, keys, values, lengths, out_weight, out_cotangent):
    Y, Z = grid
    X = chips_x
    answers = queries.shape[1]
    tokens = keys.shape[2]
    count = keys.shape[1] * tokens
    inner = keys.shape[3]
    heads = inner // 64
    model = out_weight.shape[0]
    span = inner // (X * Y)
    vmem = pltpu.VMEM

    def reduce_buffers():
        return [
            vmem((heads, 2, 32, answers), BF),
            vmem((heads, 32, answers), BF),
            vmem((heads, 32, answers), BF),
            vmem((heads - 1, 32, answers), BF),
        ]

    full = vmem((heads, 2, 32, answers), BF)
    scratch = [
        vmem((model, inner), BF),
        vmem((model, answers), BF),
        vmem((count, inner), BF),
        vmem((count, inner), BF),
        vmem((heads // 2, count, 2 * answers), BF),
        vmem((heads // 2, count, 2 * answers), BF),
        vmem((count, answers), F32),
        full, full, full, full, full, full,
        vmem((heads, 64, answers), F32),
        vmem((heads, 64, answers), F32),
        vmem((heads, 1, answers), F32),
        vmem((heads, 2, 32, answers), BF),
        vmem((heads, 2, answers), F32),
        vmem((heads, 32, answers), BF),
        vmem((heads, 2, answers), F32),
        vmem((heads, 32, answers), BF),
        vmem((heads, 2, answers), F32),
        vmem((Y - 1, Z, 32, answers), BF),
        vmem((Y - 1, Z, 2, answers), F32),
        vmem((Z, 32, answers), BF),
        vmem((Z, 2, answers), F32),
        vmem((Z - 1, 32, answers), BF),
        vmem((Z - 1, 2, answers), F32),
        vmem((heads, 2, 4, answers), F32),
        *reduce_buffers(),
        *reduce_buffers(),
        vmem((Y, X, model, span), BF),
        vmem((Y, X - 1, model, span), BF),
        vmem((Y, X, model, span), BF),
    ]
    gather = heads - 1 + Y
    scatter = Y + heads - 1
    staged = Y + (Y - 1) + (Z - 1)
    copies = 4 * gather + 2 * scatter + 2 * staged + 2 * Y * (X - 1)
    scratch += [
        pltpu.SemaphoreType.DMA((copies,)),
        pltpu.SemaphoreType.DMA((copies,)),
        pltpu.SemaphoreType.DMA((2 * Y + 3,)),
    ]
    in_vmem = pl.BlockSpec(memory_space=pltpu.VMEM)
    in_hbm = pl.BlockSpec(memory_space=pltpu.HBM)
    shapes = (
        ((model, answers), BF),
        ((model, inner), F32),
        ((queries.shape[2], answers), BF),
        ((count, inner), BF),
        ((count, inner), BF),
    )
    results = pl.pallas_call(
        functools.partial(layer_kernel, (X, Y, Z, tokens)),
        out_shape=tuple(vmem(*shape) for shape in shapes),
        in_specs=[
            in_hbm, in_hbm, in_hbm,
            pl.BlockSpec(memory_space=pltpu.SMEM),
            in_hbm, in_hbm,
        ],
        out_specs=(in_vmem,) * len(shapes),
        scratch_shapes=scratch,
        compiler_params=pltpu.CompilerParams(
            collective_id=0, has_side_effects=True, vmem_limit_bytes=50 << 20
        ),
    )(
        queries[0].T,
        keys.reshape(count, inner),
        values.reshape(count, inner),
        lengths,
        out_weight,
        out_cotangent[0].T,
    )
    layer_out, weight_grad, query_grad, key_grad, value_grad = pl.pallas_call(
        store_kernel,
        out_shape=tuple(jax.ShapeDtypeStruct(*shape) for shape in shapes),
        in_specs=[in_vmem] * len(shapes),
        out_specs=(in_hbm,) * len(shapes),
        scratch_shapes=[pltpu.SemaphoreType.DMA((len(shapes),))],
        compiler_params=pltpu.CompilerParams(vmem_limit_bytes=4 << 20),
    )(*(pltpu.with_memory_space_constraint(part, pltpu.VMEM) for part in results))
    return (
        layer_out.T[None],
        weight_grad,
        query_grad.T[None],
        key_grad.reshape(keys.shape),
        value_grad.reshape(values.shape),
    )


def solution(mesh):
    body = functools.partial(per_device, GRIDS[mesh.shape["psg"]], mesh.shape["dp"])
    return jax.shard_map(
        body,
        mesh=mesh,
        in_specs=(
            P("dp", None, "psg"),
            P("dp", "psg", None, None),
            P("dp", "psg", None, None),
            P("dp", "psg"),
            P("psg", None),
            P("dp", None, "psg"),
        ),
        out_specs=(
            P("dp", None, "psg"),
            P("psg", None),
            P("dp", None, "psg"),
            P("dp", "psg", None, None),
            P("dp", "psg", None, None),
        ),
        check_vma=False,
    )
```

```python
import functools

import jax
import jax.numpy as jnp
from jax import lax
from jax.experimental import pallas as pl
from jax.experimental.pallas import tpu as pltpu
from jax.sharding import PartitionSpec as P

BF = jnp.bfloat16
F32 = jnp.float32
MESH = pl.DeviceIdType.MESH
MASKED = -1e30
GRIDS = {64: (4, 8), 8: (2, 2)}

NN = (((1,), (0,)), ((), ()))
NT = (((1,), (1,)), ((), ()))
TN = (((0,), (0,)), ((), ()))


def dot(a, b, dims=NN):
    return lax.dot_general(a, b, dims, preferred_element_type=F32)


def block_diagonal(pair):
    zero = jnp.zeros((64, pair.shape[1]), pair.dtype)
    first = jnp.concatenate([pair[:64], zero], axis=0)
    second = jnp.concatenate([zero, pair[64:]], axis=0)
    return jnp.concatenate([first, second], axis=1)


class Wires:
    def __init__(self, send_sems, recv_sems):
        self.send_sems, self.recv_sems = send_sems, recv_sems
        self.count = 0
        self.sent = []

    def send(self, src, dst, device_id):
        copy = pltpu.make_async_remote_copy(
            src_ref=src,
            dst_ref=dst,
            send_sem=self.send_sems.at[self.count],
            recv_sem=self.recv_sems.at[self.count],
            device_id=device_id,
            device_id_type=MESH,
        )
        self.count += 1
        copy.start()
        self.sent.append(copy)
        return copy

    def finish(self, keep=0):
        count = len(self.sent) - keep
        for copy in self.sent[:count]:
            copy.wait_send()
        self.sent = self.sent[count:]


def layer_kernel(
    dims,
    q_hbm, k_hbm, v_hbm, len_ref, w_hbm, g_hbm,
    lo_ref, wg_ref, dq_ref, dkb, dvb,
    w_ref, g_ref, kb, vb, vt, pb, ub, bias,
    qb, gb, cb, fgb, fqb, fdb, ab, bb, cen,
    po, st, rco, rcs, tbo, tbs, ryo, rys, tzo, tzs, rzo, rzs, sg,
    pg, rcg, tbg, rzg,
    pd, rcd, tbd, rzd,
    wgp, rxw, wgf,
    send_sems, recv_sems, load_sems,
):
    X, Y, Z, tokens = dims
    heads = Y * Z
    keys = kb.shape[0]
    answers = qb.shape[3]
    width = Z * 64
    x = lax.axis_index("dp")
    me = lax.axis_index("psg")
    c = lax.rem(me, 2)
    chip = me // 2
    z = lax.rem(chip, Z)
    y = chip // Z

    def at_yz(dy, dz):
        return {"psg": (lax.rem(y + dy, Y) * Z + lax.rem(z + dz, Z)) * 2 + c}

    def at_z(k):
        return at_yz(0, k)

    def at_y(k):
        return at_yz(k, 0)

    def at_x(k):
        return {"dp": lax.rem(x + k, X)}

    targets = [
        (dy, dz)
        for dy in reversed(range(Y))
        for dz in sorted(range(Z), key=lambda dz: -min(dz, Z - dz))
        if (dy, dz) != (0, 0)
    ]
    partner = {"psg": chip * 2 + (1 - c)}
    wires = Wires(send_sems, recv_sems)

    def block_of(k):
        return lax.rem(y + k, Y)

    def rows(b):
        return pl.ds(b * Z, Z)

    def lanes(b):
        return pl.ds(pl.multiple_of(b * width, width), width)

    barrier = pltpu.get_barrier_semaphore()
    peers = [at_yz(*d) for d in targets] + [partner] + [at_x(k) for k in range(1, X)]
    for peer in peers:
        pl.semaphore_signal(barrier, inc=1, device_id=peer, device_id_type=MESH)

    small = []
    for n, (src, dst) in enumerate(((q_hbm, qb.at[chip, c]), (g_hbm, g_ref), (w_hbm, w_ref))):
        copy = pltpu.make_async_copy(src, dst, load_sems.at[2 * Y + n])
        copy.start()
        small.append(copy)
    loads = []
    for i in range(Y):
        b = block_of(i + 1)
        pair = []
        for n, (src, dst) in enumerate(((k_hbm, kb), (v_hbm, vb))):
            copy = pltpu.make_async_copy(
                src.at[:, lanes(b)], dst.at[:, lanes(b)], load_sems.at[2 * i + n]
            )
            copy.start()
            pair.append(copy)
        loads.append(pair)
    for copy in small:
        copy.wait()
    g_t = g_ref[...]
    pl.semaphore_wait(barrier, len(peers))

    def gather_start(buf):
        own = buf.at[chip, c]
        return {d: wires.send(own, own, at_yz(*d)) for d in targets}

    def gather_block(buf, copies, i):
        for dz in range(Z):
            if (Y - 1 - i, dz) in copies:
                copies[Y - 1 - i, dz].wait_recv()
        part = buf.at[rows(block_of(i + 1)), c]
        return wires.send(part, part, partner)

    def gather_core(buf, copies):
        return [gather_block(buf, copies, i) for i in range(Y)]

    def gather_end(core_copies):
        for copy in core_copies:
            copy.wait_recv()

    def scatter_core(part, landing, b):
        return wires.send(part.at[rows(b), 1 - c], landing.at[rows(b)], partner)

    def scatter_start(part, landing, total, pieces, core_copies):
        copies = []
        for i in range(Y):
            b = block_of(i + 1)
            core_copies[i].wait_recv()
            both = part[rows(b), c].astype(F32) + landing[rows(b)].astype(F32)
            total[rows(b)] = both.astype(BF)
            dy = (i + 1) % Y
            for dz in sorted(range(Z), key=lambda dz: -min(dz, Z - dz)):
                if (dy, dz) != (0, 0):
                    piece = total.at[b * Z + lax.rem(z + dz, Z)]
                    copies.append(
                        wires.send(piece, pieces.at[dy * Z + dz - 1], at_yz(dy, dz))
                    )
        return copies

    def scatter_end(total, pieces, copies):
        for copy in copies:
            copy.wait_recv()
        return total[chip].astype(F32) + jnp.sum(pieces[...].astype(F32), axis=0)

    q_copies = gather_start(qb)
    g_core = []
    for i in range(Y):
        b = block_of(i + 1)
        term = dot(w_ref[:, lanes(b)], g_t, TN)
        pg[rows(b)] = term.reshape(Z, 2, 32, answers).astype(BF)
        g_core.append(scatter_core(pg, rcg, b))
    for passage in range(keys // tokens):
        position = lax.broadcasted_iota(jnp.int32, (tokens, answers), 0)
        bias[passage * tokens : (passage + 1) * tokens] = jnp.where(
            position < len_ref[0, passage], 0.0, MASKED
        )
    g_pieces = scatter_start(pg, rcg, tbg, rzg, g_core)

    def columns(j):
        return pl.ds(pl.multiple_of(j * 128, 128), 128)

    def pair_of(buf, j):
        return block_diagonal(buf[pl.ds(2 * j, 2)].reshape(128, answers))

    def forward_pair(j):
        scores = dot(kb[:, columns(j)], pair_of(qb, j))
        for half in range(2):
            part = scores[:, half * answers : (half + 1) * answers] + bias[...]
            top = jnp.max(part, axis=0, keepdims=True)
            weights = jnp.exp(part - top)
            st[2 * j + half, 0:1, :] = top
            st[2 * j + half, 1:2, :] = jnp.sum(weights, axis=0, keepdims=True)
            pb[j, :, half * answers : (half + 1) * answers] = weights.astype(BF)
        out = dot(vt[columns(j), :], pb[j])
        po[2 * j] = out[:64, :answers].reshape(2, 32, answers).astype(BF)
        po[2 * j + 1] = out[64:, answers:].reshape(2, 32, answers).astype(BF)

    def run_block(body, b):
        @pl.loop(0, Z // 2, unroll=Z // 2)
        def _(i):
            body(b * (Z // 2) + i)

    def merge(terms):
        top = terms[0][1]
        for _, other, _ in terms[1:]:
            top = jnp.maximum(top, other)
        output, total = None, None
        for out, own, part in terms:
            scale = jnp.exp(own - top)
            output = out * scale if output is None else output + out * scale
            total = part * scale if total is None else total + part * scale
        return output, top, total

    def triple(out, stats):
        return out.astype(F32), stats[..., 0:1, :], stats[..., 1:2, :]

    def output_core(b):
        return scatter_core(po, rco, b), wires.send(st.at[rows(b)], rcs.at[rows(b)], partner)

    def output_y(copies, b, k):
        for copy in copies:
            copy.wait_recv()
        output, top, total = merge(
            [triple(po[rows(b), c], st[rows(b)]), triple(rco[rows(b)], rcs[rows(b)])]
        )
        tbo[rows(b)] = output.astype(BF)
        tbs[rows(b), 0:1, :] = top
        tbs[rows(b), 1:2, :] = total
        if k == Y:
            return None
        return (
            wires.send(tbo.at[rows(b)], ryo.at[k - 1], at_y(k)),
            wires.send(tbs.at[rows(b)], rys.at[k - 1], at_y(k)),
        )

    def output_z():
        terms = [triple(tbo[rows(y)], tbs[rows(y)])]
        for k in range(1, Y):
            for copy in o_y[k - 1]:
                copy.wait_recv()
            terms.append(triple(ryo[k - 1], rys[k - 1]))
        output, top, total = merge(terms)
        tzo[...] = output.astype(BF)
        tzs[:, 0:1, :] = top
        tzs[:, 1:2, :] = total
        copies = []
        for k in range(1, Z):
            t = lax.rem(z + k, Z)
            copies.append(
                (
                    wires.send(tzo.at[t], rzo.at[k - 1], at_z(k)),
                    wires.send(tzs.at[t], rzs.at[k - 1], at_z(k)),
                )
            )
        return copies

    def output_end(copies):
        terms = [triple(tzo[z], tzs[z])]
        for k in range(1, Z):
            for copy in copies[k - 1]:
                copy.wait_recv()
            terms.append(triple(rzo[k - 1], rzs[k - 1]))
        return merge(terms)

    def middle_pair(j):
        centers = []
        for half in range(2):
            h = 2 * j + half
            products = gb[h].astype(F32) * po[h].astype(F32)
            center = jnp.sum(products.reshape(64, answers), axis=0, keepdims=True) / st[h, 1:2, :]
            cen[h] = center
            centers.append(center)
        prob_grad = dot(vb[:, columns(j)], pair_of(gb, j))
        weights = pb[j]
        centered = prob_grad - jnp.concatenate(centers, axis=1)
        score_grad = (weights.astype(F32) * centered).astype(BF)
        ub[j] = score_grad
        key_pair = kb[:, columns(j)]
        for out, terms in ((ab, score_grad), (bb, weights)):
            product = dot(key_pair, terms, TN)
            out[2 * j] = product[:64, :answers]
            out[2 * j + 1] = product[64:, answers:]

    o_core, o_y = [], []
    for pair in loads:
        for copy in pair:
            copy.wait()

    @pl.loop(0, heads // 2, unroll=Z // 2)
    def _(j):
        vt[columns(j), :] = vb[:, columns(j)].T

    q_core = [gather_block(qb, q_copies, 0)]
    for i in range(Y):
        b = block_of(i + 1)
        if i + 1 < Y:
            q_core.append(gather_block(qb, q_copies, i + 1))
        q_core[i].wait_recv()
        run_block(forward_pair, b)
        o_core.append(output_core(b))
        if i > 0:
            o_y.append(output_y(o_core[i - 1], block_of(i), i))
        if i == Y - 2:
            gb[chip, c] = scatter_end(tbg, rzg, g_pieces).astype(BF)
            g_copies = gather_start(gb)
    output_y(o_core[Y - 1], y, Y)
    o_z = output_z()
    older = len(wires.sent)

    output, top, total = output_end(o_z)
    context = (output / total).astype(BF)
    cb[chip, c] = context
    sg[chip, c, 0:1, :] = top
    sg[chip, c, 1:2, :] = total
    sg[chip, c, 2:3, :] = jnp.sum(
        gb[chip, c].astype(F32) * context.astype(F32), axis=0, keepdims=True
    )
    sg[chip, c, 3:4, :] = total
    s_copies = gather_start(sg)
    c_copies = gather_start(cb)
    gather_end(gather_core(gb, g_copies))
    for b in range(Y):
        run_block(middle_pair, b)
    wires.finish(keep=len(wires.sent) - older)
    s_core = gather_core(sg, s_copies)
    gather_end(s_core)

    factors, shifts, d_core = [], [], []
    for i in range(Y):
        b = block_of(i + 1)
        stats = sg[rows(b)]
        factor = jnp.exp(st[rows(b), 0:1, :] - stats[:, 0, 0:1, :]) / stats[:, 0, 1:2, :]
        shift = factor * (stats[:, 0, 2:3, :] + stats[:, 1, 2:3, :] - cen[rows(b)])
        query_terms = factor * ab[rows(b)] - shift * bb[rows(b)]
        pd[rows(b)] = query_terms.astype(BF).reshape(Z, 2, 32, answers)
        d_core.append(scatter_core(pd, rcd, b))
        factors.append(factor)
        shifts.append(shift)

    c_core = gather_core(cb, c_copies)
    d_pieces = scatter_start(pd, rcd, tbd, rzd, d_core)

    span = width // X
    w_copies = []
    for i in range(Y):
        c_core[i].wait_recv()
        term = dot(g_t, cb[rows(block_of(i + 1))].reshape(width, answers), NT).astype(BF)
        for n in range(X):
            wgp[i, n] = term[:, n * span : (n + 1) * span]
        w_copies.append(
            [
                wires.send(wgp.at[i, lax.rem(x + k, X)], rxw.at[i, k - 1], at_x(k))
                for k in range(1, X)
            ]
        )

    for i in range(Y):
        b = block_of(i + 1)

        def scaled(buf, by):
            wide = buf[rows(b)].astype(F32).reshape(Z, 64, answers) * by
            return wide.astype(BF).reshape(Z, 2, 32, answers)

        fgb[rows(b)] = scaled(gb, factors[i])
        fqb[rows(b)] = scaled(qb, factors[i])
        fdb[rows(b)] = scaled(qb, -shifts[i])

    def backward_pair(j):
        both = jnp.concatenate([pair_of(fgb, j), pair_of(fdb, j)], axis=0)
        from_weights = dot(pb[j], both, NT)
        dvb[:, columns(j)] = from_weights[:, :128].astype(BF)
        key_grad = from_weights[:, 128:] + dot(ub[j], pair_of(fqb, j), NT)
        dkb[:, columns(j)] = key_grad.astype(BF)

    for b in range(Y // 2):
        run_block(backward_pair, b)
    sums = []
    for i in range(Y):
        b = block_of(i + 1)
        both = wgp[i, x].astype(F32)
        for k in range(1, X):
            w_copies[i][k - 1].wait_recv()
            both = both + rxw[i, k - 1].astype(F32)
        wgf[b, x] = both.astype(BF)
        sums += [wires.send(wgf.at[b, x], wgf.at[b, x], at_x(k)) for k in range(1, X)]
    for b in range(Y // 2, Y):
        run_block(backward_pair, b)
    lo_ref[...] = dot(w_ref[...], cb[...].reshape(heads * 64, answers)).astype(BF)
    wires.finish(keep=len(sums))
    dq_ref[...] = scatter_end(tbd, rzd, d_pieces).astype(BF)
    for copy in sums:
        copy.wait_recv()
    for b in range(Y):
        for n in range(X):
            at = (b * X + n) * span
            wg_ref[:, at : at + span] = wgf[b, n].astype(F32)
    wires.finish()


def store_kernel(*refs):
    count = (len(refs) - 1) // 2
    copies = [
        pltpu.make_async_copy(refs[n], refs[count + n], refs[-1].at[n]) for n in range(count)
    ]
    for copy in copies:
        copy.start()
    for copy in copies:
        copy.wait()


def per_device(grid, chips_x, queries, keys, values, lengths, out_weight, out_cotangent):
    Y, Z = grid
    X = chips_x
    answers = queries.shape[1]
    tokens = keys.shape[2]
    count = keys.shape[1] * tokens
    inner = keys.shape[3]
    heads = inner // 64
    model = out_weight.shape[0]
    span = inner // (X * Y)
    vmem = pltpu.VMEM

    def reduce_buffers():
        return [
            vmem((heads, 2, 32, answers), BF),
            vmem((heads, 32, answers), BF),
            vmem((heads, 32, answers), BF),
            vmem((heads - 1, 32, answers), BF),
        ]

    full = vmem((heads, 2, 32, answers), BF)
    scratch = [
        vmem((model, inner), BF),
        vmem((model, answers), BF),
        vmem((count, inner), BF),
        vmem((count, inner), BF),
        vmem((inner, count), BF),
        vmem((heads // 2, count, 2 * answers), BF),
        vmem((heads // 2, count, 2 * answers), BF),
        vmem((count, answers), F32),
        full, full, full, full, full, full,
        vmem((heads, 64, answers), F32),
        vmem((heads, 64, answers), F32),
        vmem((heads, 1, answers), F32),
        vmem((heads, 2, 32, answers), BF),
        vmem((heads, 2, answers), F32),
        vmem((heads, 32, answers), BF),
        vmem((heads, 2, answers), F32),
        vmem((heads, 32, answers), BF),
        vmem((heads, 2, answers), F32),
        vmem((Y - 1, Z, 32, answers), BF),
        vmem((Y - 1, Z, 2, answers), F32),
        vmem((Z, 32, answers), BF),
        vmem((Z, 2, answers), F32),
        vmem((Z - 1, 32, answers), BF),
        vmem((Z - 1, 2, answers), F32),
        vmem((heads, 2, 4, answers), F32),
        *reduce_buffers(),
        *reduce_buffers(),
        vmem((Y, X, model, span), BF),
        vmem((Y, X - 1, model, span), BF),
        vmem((Y, X, model, span), BF),
    ]
    gather = heads - 1 + Y
    scatter = Y + heads - 1
    staged = Y + (Y - 1) + (Z - 1)
    copies = 4 * gather + 2 * scatter + 2 * staged + 2 * Y * (X - 1)
    scratch += [
        pltpu.SemaphoreType.DMA((copies,)),
        pltpu.SemaphoreType.DMA((copies,)),
        pltpu.SemaphoreType.DMA((2 * Y + 3,)),
    ]
    in_vmem = pl.BlockSpec(memory_space=pltpu.VMEM)
    in_hbm = pl.BlockSpec(memory_space=pltpu.HBM)
    shapes = (
        ((model, answers), BF),
        ((model, inner), F32),
        ((queries.shape[2], answers), BF),
        ((count, inner), BF),
        ((count, inner), BF),
    )
    results = pl.pallas_call(
        functools.partial(layer_kernel, (X, Y, Z, tokens)),
        out_shape=tuple(vmem(*shape) for shape in shapes),
        in_specs=[
            in_hbm, in_hbm, in_hbm,
            pl.BlockSpec(memory_space=pltpu.SMEM),
            in_hbm, in_hbm,
        ],
        out_specs=(in_vmem,) * len(shapes),
        scratch_shapes=scratch,
        compiler_params=pltpu.CompilerParams(
            collective_id=0, has_side_effects=True, vmem_limit_bytes=50 << 20
        ),
    )(
        queries[0].T,
        keys.reshape(count, inner),
        values.reshape(count, inner),
        lengths,
        out_weight,
        out_cotangent[0].T,
    )
    layer_out, weight_grad, query_grad, key_grad, value_grad = pl.pallas_call(
        store_kernel,
        out_shape=tuple(jax.ShapeDtypeStruct(*shape) for shape in shapes),
        in_specs=[in_vmem] * len(shapes),
        out_specs=(in_hbm,) * len(shapes),
        scratch_shapes=[pltpu.SemaphoreType.DMA((len(shapes),))],
        compiler_params=pltpu.CompilerParams(vmem_limit_bytes=4 << 20),
    )(*(pltpu.with_memory_space_constraint(part, pltpu.VMEM) for part in results))
    return (
        layer_out.T[None],
        weight_grad,
        query_grad.T[None],
        key_grad.reshape(keys.shape),
        value_grad.reshape(values.shape),
    )


def solution(mesh):
    body = functools.partial(per_device, GRIDS[mesh.shape["psg"]], mesh.shape["dp"])
    return jax.shard_map(
        body,
        mesh=mesh,
        in_specs=(
            P("dp", None, "psg"),
            P("dp", "psg", None, None),
            P("dp", "psg", None, None),
            P("dp", "psg"),
            P("psg", None),
            P("dp", None, "psg"),
        ),
        out_specs=(
            P("dp", None, "psg"),
            P("psg", None),
            P("dp", None, "psg"),
            P("dp", "psg", None, None),
            P("dp", "psg", None, None),
        ),
        check_vma=False,
    )
```
